32 devices in a mesh: rad: 8 (over y, x, core), azi: 4 (over z).
Axes of the slice: x: 2, y: 2, z: 4, core: 2. Of those that a mesh axis runs over, the one named last changes fastest.
Arguments:
- positions: float32 [3, 524288], P(None, ('rad', 'azi')), may hold values from 0 to 1
- velocities: float32 [3, 524288], P(None, ('rad', 'azi')), may hold values from -3 to 3
- masses: float32 [524288], P(('rad', 'azi')), may hold values from 0.5 to 2
- neighbours: int32 [4096, 4], P(('rad', 'azi')), may hold values from 0 to 143, as said below
- shear_offsets: int32 [2, 8], replicated, may hold values from 0 to 3
- destinations: int32 [4096], P(('rad', 'azi')), may hold values from 0 to 3, as said below
- deposit_cells: int32 [2, 524288], P(None, ('rad', 'azi')), may hold values from 0 to 4095
- old_potential: float32 [512, 256], P('rad', 'azi'), may hold values from -6 to 6
Outputs:
- migrated: float32 [7, 524288], P(None, ('rad', 'azi'))
- potential: float32 [512, 256], P('rad', 'azi')
The draws below stay inside these ranges and needn't reach their ends.
Inputs may be any that keep to these rules, and one draw needn't show every extreme that they name: `neighbours`: entries index a device's table of 128 own tiles and 16 ghost tiles; the first entry of each tile's list is the tile itself, and each ghost tile is listed by some tile of every device. `destinations`: one device sends at most 32 tiles to any one azimuthal strip and a device receives at most 128 tiles; in every radial strip one azimuthal strip receives exactly 32 tiles from each device of that radial strip.
All inputs are finite; a program needn't handle non-finite values.
Results may differ from the reference program's by a relative error of at most 0.0003.
Values sent between devices are 32-bit elements; how exact they have to be, the bound alone decides.
A program may use at most 64 MiB of HBM per device.

```python
import math
import jax
import jax.numpy as jnp
from jax import lax

TILES = 128
TILE = 128
EDGE = 4
LINKS = 4
GX = 64
GY = 64
STEPS = 2
SLOT = 32
CAP = 128
PART = 524288
NX = 512
NY = 256
N_RAD = 8
N_AZI = 4


def draw_neighbours(key, part):
    devices = N_RAD * N_AZI
    lists_drawn = jax.random.randint(jax.random.fold_in(key, 11), (devices, TILES, LINKS), 0, TILES + 4 * EDGE)
    own_ids = jnp.arange(TILES, dtype=jnp.int32)
    lists_drawn = lists_drawn.at[:, :, 0].set(own_ids[None, :])
    scores = jax.random.randint(jax.random.fold_in(key, 12), (devices, TILES), 0, 1 << 20) * TILES + own_ids[None, :]
    ordering = jnp.argsort(scores, axis=1)
    chosen = ordering[:, :4 * EDGE]
    ghost_ids = TILES + jnp.arange(4 * EDGE, dtype=jnp.int32)
    device_ids = jnp.arange(devices, dtype=jnp.int32)
    lists_drawn = lists_drawn.at[device_ids[:, None], chosen, 1].set(ghost_ids[None, :])
    return lists_drawn.reshape(devices * TILES, LINKS).astype(jnp.int32)


def draw_destinations(key, part):
    slot_cap = TILES // 4
    hot_strip = jax.random.randint(jax.random.fold_in(key, 21), (N_RAD,), 0, N_AZI)
    rotation = jax.random.randint(jax.random.fold_in(key, 22), (N_RAD, N_AZI), 0, N_AZI - 1)
    tile_ids = jnp.arange(TILES, dtype=jnp.int32)
    scores = jax.random.randint(jax.random.fold_in(key, 23), (N_RAD, N_AZI, TILES), 0, 1 << 20) * TILES + tile_ids
    ranking = jnp.argsort(jnp.argsort(scores, axis=2), axis=2)
    spread = (hot_strip[:, None, None] + 1 + (ranking - slot_cap + rotation[:, :, None]) % (N_AZI - 1)) % N_AZI
    dest_strip = jnp.where(ranking < slot_cap, hot_strip[:, None, None], spread)
    return dest_strip.reshape(-1).astype(jnp.int32)


def plant(array, stream_key, least, largest):
    spot = [jax.random.randint(jax.random.fold_in(stream_key, axis), (), 0, length) for axis, length in enumerate(array.shape)]
    longest = array.shape.index(max(array.shape))
    neighbour = spot[:longest] + [(spot[longest] + 1) % array.shape[longest]] + spot[longest + 1:]
    return array.at[tuple(spot)].set(least).at[tuple(neighbour)].set(largest)


def block_levels(stream_key, extent, cuts, smallest, top_value):
    gain = 1.0
    for position, blocks in cuts:
        heights = jax.random.uniform(jax.random.fold_in(jax.random.fold_in(stream_key, 6), position), (blocks,), jnp.float32, smallest / len(cuts), top_value / len(cuts))
        gain = gain * jnp.repeat(jnp.exp(heights), extent[position] // blocks).reshape((-1,) + (1,) * (len(extent) - 1 - position))
    return gain


def gaussian(own_key, extent, scale, bound, shards=(), held_as=jnp.bfloat16):
    entries = jax.random.normal(own_key, extent, jnp.float32) * scale
    if len(shards) > 0:
        entries = block_levels(own_key, extent, shards, -0.22, 0.18) * entries
    return jnp.clip(entries, min=-bound, max=bound).astype(held_as)


def setup_inputs(seed: int = 0) -> dict:
    splits = jax.random.split(jax.random.key(seed), 9)
    return {
        "positions": jnp.clip(1.0 * jax.random.uniform(splits[0], (3, PART), jnp.float32) ** block_levels(splits[0], (3, PART), ((1, 32),), -0.2, 0.2), 0.0, 1.0),
        "velocities": gaussian(splits[1], (3, PART), 0.5, 3.0, ((1, 32),), jnp.float32),
        "masses": jnp.clip(jnp.exp(math.log(2.0) - 1.3862944 * jax.random.uniform(splits[2], (PART,), jnp.float32) ** block_levels(splits[2], (PART,), ((0, 32),), -0.2, 0.2)), 0.5, 2.0),
        "neighbours": draw_neighbours(jax.random.fold_in(splits[8], 71), 0),
        "shear_offsets": plant(jax.random.randint(splits[4], (STEPS, N_RAD), 0, N_AZI), jax.random.fold_in(splits[4], 1), 0, N_AZI - 1).astype(jnp.int32),
        "destinations": draw_destinations(jax.random.fold_in(splits[8], 71), 0),
        "deposit_cells": plant(jax.random.randint(splits[6], (STEPS, PART), 0, GX * GY), jax.random.fold_in(splits[6], 1), 0, (GX * GY) - 1).astype(jnp.int32),
        "old_potential": gaussian(splits[7], (NX, NY), 1.0, 6.0, ((0, 8), (1, 4)), jnp.float32),
    }


TIME_STEP = 0.1
ORBIT_FREQ = 0.3
CONTACT_STIFF = 0.15
INV_WIDTH = 4.0
GRAV_SCALE = 0.01


def contact_forces(own_tiles, table_all, neighbour_rows):
    groups = own_tiles.shape[1] // 4
    own_groups = jnp.transpose(own_tiles.reshape(4, groups, 4, -1), (1, 0, 2, 3))
    row_groups = neighbour_rows.reshape(groups, 4, -1)

    def one_group(group_args):
        own_part, row_part = group_args
        others = jnp.take(table_all, row_part, axis=1)
        offsets = own_part[:3, :, None, :, None] - others[:3, :, :, None, :]
        distance = jnp.sum(offsets * offsets, axis=0)
        weights = others[3][:, :, None, :] * jnp.exp(-INV_WIDTH * distance)
        return CONTACT_STIFF * jnp.sum(offsets * weights[None], axis=(2, 4))

    result = lax.map(one_group, (own_groups, row_groups))
    return jnp.transpose(result, (1, 0, 2, 3)).reshape(3, own_tiles.shape[1], -1)


def solve_potential(density):
    wave_x = jnp.arange(NX)
    wave_y = jnp.arange(NY)
    eigen_x = 4.0 * jnp.sin(jnp.pi * wave_x.astype(jnp.float32) / NX) ** 2
    eigen_y = 4.0 * jnp.sin(jnp.pi * wave_y.astype(jnp.float32) / NY) ** 2
    lam_grid = eigen_x[:, None] + eigen_y[None, :]
    at_zero = (wave_x[:, None] == 0) & (wave_y[None, :] == 0)
    green = jnp.where(at_zero, 0.0, -GRAV_SCALE / jnp.where(at_zero, 1.0, lam_grid))
    spectrum = jnp.fft.fft2(density) * green
    return jnp.real(jnp.fft.ifft2(spectrum)).astype(jnp.float32)


def per_device(device_args):
    own_tiles, table_all, neighbour_rows = device_args
    return contact_forces(own_tiles, table_all, neighbour_rows)


def reference(positions, velocities, masses, neighbours, shear_offsets, destinations, deposit_cells, old_potential):
    devices = N_RAD * N_AZI
    rad_ids = jnp.arange(N_RAD, dtype=jnp.int32)
    azi_ids = jnp.arange(N_AZI, dtype=jnp.int32)
    strip_x = (rad_ids - N_RAD // 2).astype(jnp.float32)
    place = positions.reshape(3, N_RAD, N_AZI, TILES, TILE)
    speed = velocities.reshape(3, N_RAD, N_AZI, TILES, TILE)
    mass_grid = masses.reshape(N_RAD, N_AZI, TILES, TILE)
    lists_all = neighbours.reshape(devices, TILES, LINKS)
    potential_now = old_potential
    for step_index in range(STEPS):
        cell_local = deposit_cells[step_index].reshape(N_RAD, N_AZI, TILES * TILE)
        cell_x = rad_ids[:, None, None] * GX + cell_local // GY
        cell_y = azi_ids[None, :, None] * GY + cell_local % GY
        grad_x = -(jnp.roll(potential_now, -1, 0) - jnp.roll(potential_now, 1, 0)) * 0.5
        grad_y = -(jnp.roll(potential_now, -1, 1) - jnp.roll(potential_now, 1, 1)) * 0.5
        gravity_x = grad_x[cell_x, cell_y].reshape(N_RAD, N_AZI, TILES, TILE)
        gravity_y = grad_y[cell_x, cell_y].reshape(N_RAD, N_AZI, TILES, TILE)
        density = jnp.zeros((NX, NY), jnp.float32).at[cell_x, cell_y].add(mass_grid.reshape(N_RAD, N_AZI, -1))
        next_potential = solve_potential(density)

        carried = jnp.concatenate([place, mass_grid[None]], axis=0)
        offsets_now = shear_offsets[step_index]
        below_rad = (rad_ids - 1) % N_RAD
        below_azi = (azi_ids[None, :] - offsets_now[:, None]) % N_AZI
        sheared_below = carried[:, below_rad[:, None], below_azi][:, :, :, EDGE:2 * EDGE]
        sheared_below = sheared_below.at[0].add(-1.0)
        above_rad = (rad_ids + 1) % N_RAD
        above_azi = (azi_ids[None, :] + offsets_now[above_rad][:, None]) % N_AZI
        sheared_above = carried[:, above_rad[:, None], above_azi][:, :, :, :EDGE]
        sheared_above = sheared_above.at[0].add(1.0)
        from_left = carried[:, :, (azi_ids - 1) % N_AZI][:, :, :, 3 * EDGE:4 * EDGE]
        from_left = from_left.at[1].add(-1.0)
        from_right = carried[:, :, (azi_ids + 1) % N_AZI][:, :, :, 2 * EDGE:3 * EDGE]
        from_right = from_right.at[1].add(1.0)
        table_all = jnp.concatenate([carried, sheared_below, sheared_above, from_left, from_right], axis=3)

        carried_dev = jnp.transpose(carried, (1, 2, 0, 3, 4)).reshape(devices, 4, TILES, TILE)
        table_dev = jnp.transpose(table_all, (1, 2, 0, 3, 4)).reshape(devices, 4, TILES + 4 * EDGE, TILE)
        forces = lax.map(per_device, (carried_dev, table_dev, lists_all))
        forces = jnp.transpose(forces.reshape(N_RAD, N_AZI, 3, TILES, TILE), (2, 0, 1, 3, 4))

        tidal_x = place[0] + strip_x[:, None, None, None]
        accel = jnp.stack([
            forces[0] + gravity_x + 2.0 * ORBIT_FREQ * speed[1] + 3.0 * ORBIT_FREQ ** 2 * tidal_x,
            forces[1] + gravity_y - 2.0 * ORBIT_FREQ * speed[0],
            forces[2] - ORBIT_FREQ ** 2 * (place[2] - 0.5)])
        speed = speed + TIME_STEP * accel
        place = place + TIME_STEP * speed
        potential_now = next_potential

    final_state = jnp.concatenate([place, speed, mass_grid[None]], axis=0)
    dest_strip = destinations.reshape(N_RAD, N_AZI, TILES)
    hit_table = (dest_strip[..., None] == azi_ids).astype(jnp.int32)
    earlier = jnp.cumsum(hit_table, axis=2) - hit_table
    rank_slot = jnp.sum(earlier * hit_table, axis=3)
    signed = ((azi_ids[None, :, None] - dest_strip + N_AZI // 2) % N_AZI) - N_AZI // 2
    final_state = final_state.at[1].add(signed.astype(jnp.float32)[..., None])
    target = (rad_ids[:, None, None] * N_AZI + dest_strip) * CAP + azi_ids[None, :, None] * SLOT + rank_slot
    migrated = jnp.zeros((7, devices * CAP, TILE), jnp.float32)
    migrated = migrated.at[:, target.reshape(-1)].set(final_state.reshape(7, -1, TILE))
    return migrated.reshape(7, -1), potential_now
```

```python
import functools
import math

import jax
import jax.numpy as jnp
import numpy as np
from jax import lax
from jax.experimental import pallas as pl
from jax.experimental.pallas import tpu as pltpu
from jax.sharding import PartitionSpec as P

EDGE = 4
LINKS = 4
STEPS = 2
TIME_STEP = 0.1
ORBIT_FREQ = 0.3
CONTACT_STIFF = 0.15
INV_WIDTH = 4.0
GRAV_SCALE = 0.01
SCALE = math.sqrt(INV_WIDTH * math.log2(math.e))
MESH = pl.DeviceIdType.MESH
VMEM = pl.BlockSpec(memory_space=pltpu.VMEM)
SMEM = pl.BlockSpec(memory_space=pltpu.SMEM)


def real_basis(length):
    half = length // 2
    waves = np.concatenate([np.arange(half + 1), np.arange(1, half)])
    phase = (waves[:, None] * np.arange(length)[None, :]) % length
    angle = phase * (2.0 * np.pi / length)
    rows = np.where(np.arange(length)[:, None] <= half, np.cos(angle), np.sin(angle))
    norm = np.where((waves == 0) | (waves == half), 1.0, 2.0)
    return rows * np.sqrt(norm / length)[:, None], waves


def split_two(value):
    high = value.astype(jnp.bfloat16).astype(jnp.float32)
    return high, value - high


def cell_parts(cells, grid_y):
    if grid_y & (grid_y - 1) == 0:
        bits = grid_y.bit_length() - 1
        return lax.shift_right_logical(cells, bits), cells & (grid_y - 1)
    return cells // grid_y, cells % grid_y


def one_hot(ids, rows):
    return lax.broadcasted_iota(jnp.int32, (rows, ids.shape[1]), 0) == ids


def last_dims(left, right):
    return lax.dot_general(
        left, right, (((1,), (1,)), ((), ())), preferred_element_type=jnp.float32
    )


def density_kernel(grid_x, grid_y, chunk, cells_ref, mass_ref, out_ref):
    count = mass_ref.shape[1] // chunk

    def body(index, sums):
        at = pl.ds(pl.multiple_of(index * chunk, chunk), chunk)
        high, low = split_two(mass_ref[:, at])
        new = []
        for step in range(STEPS):
            cell_x, cell_y = cell_parts(cells_ref[step : step + 1, at], grid_y)
            hit = one_hot(cell_x, grid_x)
            left = jnp.concatenate(
                [jnp.where(hit, high, 0.0), jnp.where(hit, low, 0.0)], axis=0
            ).astype(jnp.bfloat16)
            right = jnp.where(one_hot(cell_y, grid_y), 1.0, 0.0).astype(jnp.bfloat16)
            new.append(sums[step] + last_dims(left, right))
        return tuple(new)

    zero = jnp.zeros((2 * grid_x, grid_y), jnp.float32)
    sums = lax.fori_loop(0, count, body, (zero,) * STEPS)
    for step in range(STEPS):
        out_ref[step] = sums[step][:grid_x] + sums[step][grid_x:]


def densities(cells, mass_row, grid_x, grid_y):
    return pl.pallas_call(
        functools.partial(density_kernel, grid_x, grid_y, 1024),
        out_shape=jax.ShapeDtypeStruct((STEPS, grid_x, grid_y), jnp.float32),
        in_specs=[VMEM, VMEM],
        out_specs=VMEM,
        name="deposit",
        cost_estimate=pl.CostEstimate(flops=4 * 10**8, bytes_accessed=3 * 10**5, transcendentals=0),
    )(cells, mass_row)


def exchange_kernel(rad_count, azi_count, edges_ref, out_ref, send_sem, recv_sem):
    rad = lax.axis_index("rad")
    azi = lax.axis_index("azi")
    above = lax.rem(rad + 1, rad_count)
    below = lax.rem(rad + rad_count - 1, rad_count)
    right = lax.rem(azi + 1, azi_count)
    left = lax.rem(azi + azi_count - 1, azi_count)
    partners = [(above, other) for other in range(azi_count)]
    partners += [(below, other) for other in range(azi_count)]
    partners += [(rad, right), (rad, left)]
    barrier = pltpu.get_barrier_semaphore()
    for partner in partners:
        pl.semaphore_signal(barrier, inc=1, device_id=partner, device_id_type=MESH)
    pl.semaphore_wait(barrier, len(partners))
    copies = []
    for index, partner in enumerate(partners):
        if index < azi_count:
            source, slot = 0, azi
        elif index < 2 * azi_count:
            source, slot = 1, azi_count + azi
        else:
            source = slot = index - 2 * azi_count
            source, slot = 2 + source, 2 * azi_count + slot
        copy = pltpu.make_async_remote_copy(
            src_ref=edges_ref.at[source],
            dst_ref=out_ref.at[slot],
            send_sem=send_sem.at[index],
            recv_sem=recv_sem.at[slot],
            device_id=partner,
            device_id_type=MESH,
        )
        copy.start()
        copies.append(copy)
    for index, partner in enumerate(partners):
        pltpu.make_async_remote_copy(
            src_ref=edges_ref.at[0],
            dst_ref=out_ref.at[index],
            send_sem=send_sem.at[index],
            recv_sem=recv_sem.at[index],
            device_id=partner,
            device_id_type=MESH,
        ).wait_recv()
    for copy in copies:
        copy.wait_send()


def exchange(edges, rad_count, azi_count, ident):
    slots = 2 * azi_count + 2
    return pl.pallas_call(
        functools.partial(exchange_kernel, rad_count, azi_count),
        out_shape=jax.ShapeDtypeStruct((slots,) + edges.shape[1:], jnp.float32),
        in_specs=[VMEM],
        out_specs=VMEM,
        scratch_shapes=[pltpu.SemaphoreType.DMA((slots,)), pltpu.SemaphoreType.DMA((slots,))],
        compiler_params=pltpu.CompilerParams(collective_id=ident, has_side_effects=True),
        name=f"exchange_{ident}",
        cost_estimate=pl.CostEstimate(flops=0, bytes_accessed=10**7, transcendentals=0),
    )(edges)


def migrate_kernel(azi_count, packed_ref, out_ref, send_sem, recv_sem, local_sem):
    rad = lax.axis_index("rad")
    azi = lax.axis_index("azi")
    width = packed_ref.shape[1] // azi_count
    others = [lax.rem(azi + hop, azi_count) for hop in range(1, azi_count)]
    barrier = pltpu.get_barrier_semaphore()
    for other in others:
        pl.semaphore_signal(barrier, inc=1, device_id=(rad, other), device_id_type=MESH)
    pl.semaphore_wait(barrier, len(others))
    mine = pl.ds(pl.multiple_of(azi * width, width), width)
    copies = []
    for index, other in enumerate(others):
        theirs = pl.ds(pl.multiple_of(other * width, width), width)
        copy = pltpu.make_async_remote_copy(
            src_ref=packed_ref.at[:, theirs],
            dst_ref=out_ref.at[:, mine],
            send_sem=send_sem.at[index],
            recv_sem=recv_sem.at[index],
            device_id=(rad, other),
            device_id_type=MESH,
        )
        copy.start()
        copies.append(copy)
    own = pltpu.make_async_copy(packed_ref.at[:, mine], out_ref.at[:, mine], local_sem)
    own.start()
    own.wait()
    for copy in copies:
        copy.wait()


def migrate(packed, azi_count, ident):
    return pl.pallas_call(
        functools.partial(migrate_kernel, azi_count),
        out_shape=jax.ShapeDtypeStruct(packed.shape, jnp.float32),
        in_specs=[VMEM],
        out_specs=VMEM,
        scratch_shapes=[
            pltpu.SemaphoreType.DMA((azi_count - 1,)),
            pltpu.SemaphoreType.DMA((azi_count - 1,)),
            pltpu.SemaphoreType.DMA,
        ],
        compiler_params=pltpu.CompilerParams(collective_id=ident, has_side_effects=True),
        name="migrate",
        cost_estimate=pl.CostEstimate(flops=0, bytes_accessed=4 * 10**7, transcendentals=0),
    )(packed)


def step_kernel(
    step, azi_count, rad_count, tile_count, grid_y, last, unroll,
    nbr_ref, slot_ref, target_ref, pos_ref, vel_ref, mass_ref, recv_ref, cells_ref, field_ref,
    *rest,
):
    if last:
        out_ref, table_ref, terms_ref, field_two_ref = rest
    else:
        pos_out, vel_out, table_ref, terms_ref, field_two_ref = rest
    tile = pos_ref.shape[1] // tile_count
    strip_x = (lax.axis_index("rad") - rad_count // 2).astype(jnp.float32)
    grid_x = field_ref.shape[1]
    high, low = split_two(field_ref[...])
    field_two_ref[...] = jnp.concatenate([high, low], axis=1).astype(jnp.bfloat16)
    if last:
        out_ref[...] = jnp.zeros_like(out_ref)

    def enter(index, place, mass):
        table_ref[index] = jnp.concatenate(
            [place * SCALE, jnp.zeros((5, tile), jnp.float32)], axis=0
        )
        rows = jnp.concatenate([mass, place * mass], axis=0)
        first = rows.astype(jnp.bfloat16).astype(jnp.float32)
        second = (rows - first).astype(jnp.bfloat16).astype(jnp.float32)
        third = rows - first - second
        terms_ref[index] = jnp.concatenate(
            [first, second, third, jnp.zeros((4, tile), jnp.float32)], axis=0
        ).astype(jnp.bfloat16)

    def own_entry(index, carry):
        at = pl.ds(pl.multiple_of(index * tile, tile), tile)
        enter(index, pos_ref[:, at], mass_ref[:, at])
        return carry

    lax.fori_loop(0, tile_count, own_entry, 0, unroll=4)
    axis_ids = lax.broadcasted_iota(jnp.int32, (3, tile), 0)
    shifts = ((0, -1.0), (0, 1.0), (1, -1.0), (1, 1.0))
    for side, (axis, amount) in enumerate(shifts):
        slot = slot_ref[side]
        for part in range(EDGE):
            block = recv_ref[slot, 0:4, part * tile : (part + 1) * tile]
            shift = jnp.where(axis_ids == axis, amount, 0.0)
            enter(tile_count + side * EDGE + part, block[0:3] + shift, block[3:4])

    def one_tile(index):
        at = pl.ds(pl.multiple_of(index * tile, tile), tile)
        turned = jnp.transpose(table_ref[index])
        own = [jnp.broadcast_to(turned[:, axis : axis + 1], (tile, tile)) for axis in range(3)]
        weights, terms = [], []
        for link in range(LINKS):
            other = nbr_ref[index * LINKS + link]
            rows = table_ref[other]
            terms.append(terms_ref[other])
            d_x = own[0] - rows[0:1]
            d_y = own[1] - rows[1:2]
            d_z = own[2] - rows[2:3]
            squares = d_x * d_x + d_y * d_y + d_z * d_z
            weights.append(jnp.exp2(-squares).astype(jnp.bfloat16))
        sums = last_dims(jnp.concatenate(terms, axis=1), jnp.concatenate(weights, axis=1))
        sums = sums[0:4] + sums[4:8] + sums[8:12]
        place = pos_ref[:, at]
        speed = vel_ref[:, at]
        force = CONTACT_STIFF * (place * sums[0:1] - sums[1:4])

        cell_x, cell_y = cell_parts(cells_ref[step : step + 1, at], grid_y)
        hit = jnp.where(one_hot(cell_x, grid_x), 1.0, 0.0).astype(jnp.bfloat16)
        lines = jnp.dot(
            field_two_ref[...], jnp.concatenate([hit, hit], axis=0),
            preferred_element_type=jnp.float32,
        )
        pick = one_hot(cell_y, grid_y)
        gravity_x = jnp.sum(jnp.where(pick, lines[:grid_y], 0.0), axis=0, keepdims=True)
        gravity_y = jnp.sum(jnp.where(pick, lines[grid_y:], 0.0), axis=0, keepdims=True)
        accel = jnp.concatenate(
            [
                force[0:1]
                + gravity_x
                + 2.0 * ORBIT_FREQ * speed[1:2]
                + 3.0 * ORBIT_FREQ**2 * (place[0:1] + strip_x),
                force[1:2] + gravity_y - 2.0 * ORBIT_FREQ * speed[0:1],
                force[2:3] - ORBIT_FREQ**2 * (place[2:3] - 0.5),
            ],
            axis=0,
        )
        speed = speed + TIME_STEP * accel
        place = place + TIME_STEP * speed
        return at, place, speed

    def body(group, carry):
        for part in range(unroll):
            index = group * unroll + part
            at, place, speed = one_tile(index)
            if last:
                azi = lax.axis_index("azi")
                strip = nbr_ref[tile_count * LINKS + index]
                moved = lax.rem(azi - strip + azi_count + azi_count // 2, azi_count)
                moved = (moved - azi_count // 2).astype(jnp.float32)
                place = place + jnp.where(axis_ids == 1, moved, 0.0)
                to = pl.ds(pl.multiple_of(target_ref[index] * tile, tile), tile)
                out_ref[:, to] = jnp.concatenate([place, speed, mass_ref[:, at]], axis=0)
            else:
                pos_out[:, at] = place
                vel_out[:, at] = speed
        return carry

    lax.fori_loop(0, tile_count // unroll, body, 0)


def advance(step, counts, tile_count, grid_y, slots_out, numbers, slot_ids, target,
            place, speed, mass_row, received, cells, field):
    rad_count, azi_count = counts
    last = step == STEPS - 1
    tile = place.shape[1] // tile_count
    if last:
        out_shape = jax.ShapeDtypeStruct((7, slots_out * tile), jnp.float32)
        out_specs = VMEM
    else:
        out_shape = (jax.ShapeDtypeStruct(place.shape, jnp.float32),) * 2
        out_specs = (VMEM, VMEM)
    return pl.pallas_call(
        functools.partial(
            step_kernel, step, azi_count, rad_count, tile_count, grid_y, last, 2
        ),
        out_shape=out_shape,
        in_specs=[SMEM] * 3 + [VMEM] * 6,
        out_specs=out_specs,
        scratch_shapes=[
            pltpu.VMEM((tile_count + 4 * EDGE, 8, tile), jnp.float32),
            pltpu.VMEM((tile_count + 4 * EDGE, 16, tile), jnp.bfloat16),
            pltpu.VMEM((field.shape[0], 2 * field.shape[1]), jnp.bfloat16),
        ],
        name=f"advance_{step}",
        cost_estimate=pl.CostEstimate(
            flops=3 * 10**8, bytes_accessed=5 * 10**7, transcendentals=8 * 10**6
        ),
    )(numbers, slot_ids, target, place, speed, mass_row, received, cells, field)


def exact(left, right):
    return jnp.dot(left, right, precision=lax.Precision.HIGHEST)


def solve(density, rad_place, azi_place, rad_count, azi_count):
    _, grid_x, grid_y = density.shape
    size_x, size_y = grid_x * rad_count, grid_y * azi_count
    peers = rad_count * azi_count
    rows = size_y // peers
    basis_x, waves_x = real_basis(size_x)
    basis_y, waves_y = real_basis(size_y)
    slope_y = -0.5 * (np.roll(basis_y, -1, axis=1) - np.roll(basis_y, 1, axis=1))
    table_x = jnp.asarray(basis_x, jnp.float32)
    table_y = jnp.asarray(np.stack([basis_y.T, slope_y.T]), jnp.float32)
    own_y = lax.dynamic_slice_in_dim(table_y, azi_place * grid_y, grid_y, axis=1)
    flat = density.reshape(STEPS * grid_x, grid_y)
    partial = lax.dot_general(
        own_y[0], flat, (((0,), (1,)), ((), ())), precision=lax.Precision.HIGHEST
    )
    partial = partial.reshape(peers, rows, STEPS * grid_x)
    got = lax.all_to_all(partial, ("rad", "azi"), split_axis=0, concat_axis=0, tiled=True)
    lines = got.reshape(rad_count, azi_count, rows, STEPS, grid_x).sum(axis=1)
    lines = jnp.transpose(lines, (2, 1, 0, 3)).reshape(STEPS * rows, size_x)
    spectrum = lax.dot_general(
        lines, table_x, (((1,), (1,)), ((), ())), precision=lax.Precision.HIGHEST
    )
    eigen_x = jnp.asarray(4.0 * np.sin(np.pi * waves_x / size_x) ** 2, jnp.float32)
    eigen_y = jnp.asarray(4.0 * np.sin(np.pi * waves_y / size_y) ** 2, jnp.float32)
    own_eigen = lax.dynamic_slice_in_dim(
        eigen_y, (rad_place * azi_count + azi_place) * rows, rows, axis=0
    )
    total = eigen_x[None, :] + own_eigen[:, None]
    green = jnp.where(total == 0.0, 0.0, -GRAV_SCALE / jnp.where(total == 0.0, 1.0, total))
    spectrum = spectrum.reshape(STEPS, rows, size_x) * green[None]
    lines = exact(spectrum.reshape(STEPS * rows, size_x), table_x).reshape(STEPS, rows, size_x)
    slope = -0.5 * (jnp.roll(lines[0], -1, axis=1) - jnp.roll(lines[0], 1, axis=1))
    sent = jnp.concatenate([slope[None], lines], axis=0)
    sent = sent.reshape(STEPS + 1, rows, rad_count, grid_x)
    sent = jnp.transpose(sent, (2, 1, 0, 3)).reshape(rad_count, 1, rows, (STEPS + 1) * grid_x)
    sent = jnp.broadcast_to(sent, (rad_count, azi_count, rows, (STEPS + 1) * grid_x))
    sent = sent.reshape(peers, rows, (STEPS + 1) * grid_x)
    got = lax.all_to_all(sent, ("rad", "azi"), split_axis=0, concat_axis=0, tiled=True)
    got = got.reshape(size_y, (STEPS + 1) * grid_x)
    field = jnp.concatenate(
        [exact(own_y[0], got[:, :grid_x]), exact(own_y[1], got[:, grid_x : 2 * grid_x])], axis=0
    )
    final = exact(own_y[0], got[:, 2 * grid_x :]).T
    return field, final


def local(
    positions,
    velocities,
    masses,
    neighbours,
    shear_offsets,
    destinations,
    deposit_cells,
    old_potential,
):
    rad_count = lax.axis_size("rad")
    azi_count = lax.axis_size("azi")
    rad_place = lax.axis_index("rad")
    azi_place = lax.axis_index("azi")
    tile_count = neighbours.shape[0]
    tile = positions.shape[1] // tile_count
    grid_x, grid_y = old_potential.shape
    mass_row = masses[None]
    density = densities(deposit_cells, mass_row, grid_x, grid_y)

    span = EDGE * tile

    def edges_of(place, extra):
        head = jnp.concatenate([place[:, : 4 * span], mass_row[:, : 4 * span]], axis=0)
        sides = [head[:, side * span : (side + 1) * span] for side in (1, 0, 3, 2)]
        edges = jnp.stack(sides)
        if extra is not None:
            lines = [jnp.pad(line, (0, span - line.shape[0])) for line in extra]
            lines = jnp.stack(lines)[:, None]
            edges = jnp.concatenate(
                [edges, lines, jnp.zeros((4, 3, span), jnp.float32)], axis=1
            )
        return edges

    outer = (old_potential[-1], old_potential[0], old_potential[:, -1], old_potential[:, 0])
    received = exchange(edges_of(positions, outer), rad_count, azi_count, 0)
    before = lax.dynamic_index_in_dim(received, azi_place, 0, False)[4, :grid_y]
    after = lax.dynamic_index_in_dim(received, azi_count + azi_place, 0, False)[4, :grid_y]
    left = received[2 * azi_count, 4, :grid_x]
    right = received[2 * azi_count + 1, 4, :grid_x]
    tall = jnp.concatenate([before[None], old_potential, after[None]], axis=0)
    wide = jnp.concatenate([left[:, None], old_potential, right[:, None]], axis=1)
    grad_x = -(tall[2:] - tall[:-2]) * 0.5
    grad_y = -(wide[:, 2:] - wide[:, :-2]) * 0.5
    field = jnp.concatenate([grad_x.T, grad_y.T], axis=0)

    slot_cap = tile_count // 4
    slots_out = slot_cap * azi_count
    tile_ids = jnp.arange(tile_count, dtype=jnp.int32)
    sooner = (tile_ids[None, :] < tile_ids[:, None]) & (
        destinations[None, :] == destinations[:, None]
    )
    rank = jnp.sum(sooner.astype(jnp.int32), axis=1)
    target = destinations * slot_cap + rank
    numbers = jnp.concatenate([neighbours.reshape(-1), destinations])

    def slots_of(step):
        offsets = shear_offsets[step]
        shift_below = offsets[rad_place]
        shift_above = offsets[(rad_place + 1) % rad_count]
        return jnp.stack(
            [
                (azi_place - shift_below) % azi_count,
                azi_count + (azi_place + shift_above) % azi_count,
                jnp.int32(2 * azi_count),
                jnp.int32(2 * azi_count + 1),
            ]
        )

    counts = (rad_count, azi_count)
    place, speed = advance(
        0, counts, tile_count, grid_y, slots_out, numbers, slots_of(0), target,
        positions, velocities, mass_row, received, deposit_cells, field,
    )
    field, final = solve(density, rad_place, azi_place, rad_count, azi_count)
    received = exchange(edges_of(place, None), rad_count, azi_count, 1)
    packed = advance(
        1, counts, tile_count, grid_y, slots_out, numbers, slots_of(1), target,
        place, speed, mass_row, received, deposit_cells, field,
    )
    return (migrate(packed, azi_count, 2), final)


def solution(mesh):
    placed = (
        P(None, ("rad", "azi")),
        P(None, ("rad", "azi")),
        P(("rad", "azi")),
        P(("rad", "azi"), None),
        P(),
        P(("rad", "azi")),
        P(None, ("rad", "azi")),
        P("rad", "azi"),
    )
    return jax.shard_map(
        local,
        mesh=mesh,
        in_specs=placed,
        out_specs=(P(None, ("rad", "azi")), P("rad", "azi")),
        check_vma=False,
    )
```

```python
import functools
import math

import jax
import jax.numpy as jnp
import numpy as np
from jax import lax
from jax.experimental import pallas as pl
from jax.experimental.pallas import tpu as pltpu
from jax.sharding import PartitionSpec as P

EDGE = 4
LINKS = 4
STEPS = 2
TIME_STEP = 0.1
ORBIT_FREQ = 0.3
CONTACT_STIFF = 0.15
INV_WIDTH = 4.0
GRAV_SCALE = 0.01
SCALE = math.sqrt(INV_WIDTH * math.log2(math.e))
UNROLL = 8
MESH = pl.DeviceIdType.MESH
VMEM = pl.BlockSpec(memory_space=pltpu.VMEM)
SMEM = pl.BlockSpec(memory_space=pltpu.SMEM)


def real_basis(length):
    half = length // 2
    waves = np.concatenate([np.arange(half + 1), np.arange(1, half)])
    phase = (waves[:, None] * np.arange(length)[None, :]) % length
    angle = phase * (2.0 * np.pi / length)
    rows = np.where(np.arange(length)[:, None] <= half, np.cos(angle), np.sin(angle))
    norm = np.where((waves == 0) | (waves == half), 1.0, 2.0)
    return rows * np.sqrt(norm / length)[:, None], waves


def split_two(value):
    high = value.astype(jnp.bfloat16).astype(jnp.float32)
    return high, value - high


def cell_parts(cells, grid_y):
    if grid_y & (grid_y - 1) == 0:
        bits = grid_y.bit_length() - 1
        return lax.shift_right_logical(cells, bits), cells & (grid_y - 1)
    return cells // grid_y, cells % grid_y


def one_hot(ids, rows):
    return lax.broadcasted_iota(jnp.int32, (rows, ids.shape[1]), 0) == ids


def last_dims(left, right):
    return lax.dot_general(
        left, right, (((1,), (1,)), ((), ())), preferred_element_type=jnp.float32
    )


def density_kernel(
    counts, grid_x, grid_y, chunk, cells_ref, mass_ref, edges_ref, out_ref, recv_ref, *sems
):
    count = mass_ref.shape[1] // chunk
    edges = Edges(*counts, edges_ref, recv_ref, *sems)
    edges.greet()

    def body(index, sums):
        at = pl.ds(pl.multiple_of(index * chunk, chunk), chunk)
        high, low = split_two(mass_ref[:, at])
        new = []
        for step in range(STEPS):
            cell_x, cell_y = cell_parts(cells_ref[step : step + 1, at], grid_y)
            hit = one_hot(cell_x, grid_x)
            left = jnp.concatenate(
                [jnp.where(hit, high, 0.0), jnp.where(hit, low, 0.0)], axis=0
            ).astype(jnp.bfloat16)
            right = jnp.where(one_hot(cell_y, grid_y), 1.0, 0.0).astype(jnp.bfloat16)
            new.append(sums[step] + last_dims(left, right))
        return tuple(new)

    zero = jnp.zeros((2 * grid_x, grid_y), jnp.float32)
    sums = lax.fori_loop(0, count // 4, body, (zero,) * STEPS)
    edges.start()
    sums = lax.fori_loop(count // 4, count, body, sums)
    for step in range(STEPS):
        out_ref[step] = sums[step][:grid_x] + sums[step][grid_x:]
    edges.finish()


def densities(cells, mass_row, edges, counts, grid_x, grid_y):
    slots = 2 * counts[1] + 2
    return pl.pallas_call(
        functools.partial(density_kernel, counts, grid_x, grid_y, 1024),
        out_shape=(
            jax.ShapeDtypeStruct((STEPS, grid_x, grid_y), jnp.float32),
            jax.ShapeDtypeStruct((slots,) + edges.shape[1:], jnp.float32),
        ),
        in_specs=[VMEM, VMEM, VMEM],
        out_specs=(VMEM, VMEM),
        scratch_shapes=edge_sems(slots),
        compiler_params=pltpu.CompilerParams(collective_id=0, has_side_effects=True),
        name="deposit",
        cost_estimate=pl.CostEstimate(flops=4 * 10**8, bytes_accessed=3 * 10**5, transcendentals=0),
    )(cells, mass_row, edges)


def exchange_kernel(counts, edges_ref, out_ref, *sems):
    edges = Edges(*counts, edges_ref, out_ref, *sems)
    edges.greet()
    edges.start()
    edges.finish()


def exchange(edges, counts, ident):
    slots = 2 * counts[1] + 2
    return pl.pallas_call(
        functools.partial(exchange_kernel, counts),
        out_shape=jax.ShapeDtypeStruct((slots,) + edges.shape[1:], jnp.float32),
        in_specs=[VMEM],
        out_specs=VMEM,
        scratch_shapes=edge_sems(slots),
        compiler_params=pltpu.CompilerParams(collective_id=ident, has_side_effects=True),
        name="exchange",
        cost_estimate=pl.CostEstimate(flops=0, bytes_accessed=10**7, transcendentals=0),
    )(edges)


class Edges:
    def __init__(self, rad_count, azi_count, edges_ref, out_ref, send_sem, recv_sem):
        rad, azi = lax.axis_index("rad"), lax.axis_index("azi")
        above = lax.rem(rad + 1, rad_count)
        below = lax.rem(rad + rad_count - 1, rad_count)
        right = lax.rem(azi + 1, azi_count)
        left = lax.rem(azi + azi_count - 1, azi_count)
        self.partners = [(above, other) for other in range(azi_count)]
        self.partners += [(below, other) for other in range(azi_count)]
        self.partners += [(rad, right), (rad, left)]
        self.copies = []
        for index, partner in enumerate(self.partners):
            if index < azi_count:
                source, slot = 0, azi
            elif index < 2 * azi_count:
                source, slot = 1, azi_count + azi
            else:
                source, slot = 2 + index - 2 * azi_count, index
            self.copies.append(
                pltpu.make_async_remote_copy(
                    src_ref=edges_ref.at[source],
                    dst_ref=out_ref.at[slot],
                    send_sem=send_sem.at[index],
                    recv_sem=recv_sem.at[slot],
                    device_id=partner,
                    device_id_type=MESH,
                )
            )
        self.arrivals = [
            pltpu.make_async_remote_copy(
                src_ref=edges_ref.at[0],
                dst_ref=out_ref.at[index],
                send_sem=send_sem.at[index],
                recv_sem=recv_sem.at[index],
                device_id=partner,
                device_id_type=MESH,
            )
            for index, partner in enumerate(self.partners)
        ]

    def greet(self):
        barrier = pltpu.get_barrier_semaphore()
        for partner in self.partners:
            pl.semaphore_signal(barrier, inc=1, device_id=partner, device_id_type=MESH)

    def start(self):
        pl.semaphore_wait(pltpu.get_barrier_semaphore(), len(self.partners))
        for copy in self.copies:
            copy.start()

    def finish(self):
        for arrival in self.arrivals:
            arrival.wait_recv()
        for copy in self.copies:
            copy.wait_send()


def edge_sems(slots):
    return [pltpu.SemaphoreType.DMA((slots,)), pltpu.SemaphoreType.DMA((slots,))]


def migrate_kernel(azi_count, packed_ref, out_ref, send_sem, recv_sem, local_sem):
    rad = lax.axis_index("rad")
    azi = lax.axis_index("azi")
    width = packed_ref.shape[1] // azi_count
    others = [lax.rem(azi + hop, azi_count) for hop in range(1, azi_count)]
    barrier = pltpu.get_barrier_semaphore()
    for other in others:
        pl.semaphore_signal(barrier, inc=1, device_id=(rad, other), device_id_type=MESH)
    pl.semaphore_wait(barrier, len(others))
    mine = pl.ds(pl.multiple_of(azi * width, width), width)
    copies = []
    for index, other in enumerate(others):
        theirs = pl.ds(pl.multiple_of(other * width, width), width)
        copy = pltpu.make_async_remote_copy(
            src_ref=packed_ref.at[:, theirs],
            dst_ref=out_ref.at[:, mine],
            send_sem=send_sem.at[index],
            recv_sem=recv_sem.at[index],
            device_id=(rad, other),
            device_id_type=MESH,
        )
        copy.start()
        copies.append(copy)
    own = pltpu.make_async_copy(packed_ref.at[:, mine], out_ref.at[:, mine], local_sem)
    own.start()
    own.wait()
    for copy in copies:
        copy.wait()


def migrate(packed, azi_count, ident):
    return pl.pallas_call(
        functools.partial(migrate_kernel, azi_count),
        out_shape=jax.ShapeDtypeStruct(packed.shape, jnp.float32),
        in_specs=[VMEM],
        out_specs=VMEM,
        scratch_shapes=[
            pltpu.SemaphoreType.DMA((azi_count - 1,)),
            pltpu.SemaphoreType.DMA((azi_count - 1,)),
            pltpu.SemaphoreType.DMA,
        ],
        compiler_params=pltpu.CompilerParams(collective_id=ident, has_side_effects=True),
        name="migrate",
        cost_estimate=pl.CostEstimate(flops=0, bytes_accessed=4 * 10**7, transcendentals=0),
    )(packed)


def step_kernel(
    step, azi_count, rad_count, tile_count, grid_y, last, unroll,
    nbr_ref, slot_ref, target_ref, pos_ref, vel_ref, mass_ref, recv_ref, cells_ref, field_ref,
    *rest,
):
    tile = pos_ref.shape[1] // tile_count
    rad, azi = lax.axis_index("rad"), lax.axis_index("azi")
    if last:
        out_ref, table_ref, terms_ref, field_two_ref = rest
    else:
        pos_out, vel_out, table_ref, terms_ref, field_two_ref = rest
    strip_x = (rad - rad_count // 2).astype(jnp.float32)
    grid_x = field_ref.shape[1]
    high, low = split_two(field_ref[...])
    field_two_ref[...] = jnp.concatenate([high, low], axis=1).astype(jnp.bfloat16)
    if last:
        out_ref[...] = jnp.zeros_like(out_ref)

    def enter(index, place, mass):
        scaled = place * SCALE
        table_ref[index] = jnp.concatenate(
            [
                scaled,
                -jnp.sum(scaled * scaled, axis=0, keepdims=True),
                scaled + scaled,
                jnp.zeros((1, tile), jnp.float32),
            ],
            axis=0,
        )
        rows = jnp.concatenate([mass, place * mass], axis=0)
        first = rows.astype(jnp.bfloat16).astype(jnp.float32)
        second = (rows - first).astype(jnp.bfloat16).astype(jnp.float32)
        third = rows - first - second
        terms_ref[index] = jnp.concatenate(
            [first, second, third, jnp.zeros((4, tile), jnp.float32)], axis=0
        ).astype(jnp.bfloat16)

    def own_entry(index, carry):
        at = pl.ds(pl.multiple_of(index * tile, tile), tile)
        enter(index, pos_ref[:, at], mass_ref[:, at])
        return carry

    lax.fori_loop(0, tile_count, own_entry, 0, unroll=4)
    axis_ids = lax.broadcasted_iota(jnp.int32, (3, tile), 0)
    shifts = ((0, -1.0), (0, 1.0), (1, -1.0), (1, 1.0))
    for side, (axis, amount) in enumerate(shifts):
        slot = slot_ref[side]
        for part in range(EDGE):
            block = recv_ref[slot, 0:4, part * tile : (part + 1) * tile]
            shift = jnp.where(axis_ids == axis, amount, 0.0)
            enter(tile_count + side * EDGE + part, block[0:3] + shift, block[3:4])

    def one_tile(index):
        at = pl.ds(pl.multiple_of(index * tile, tile), tile)
        turned = jnp.transpose(table_ref[index])
        own = [jnp.broadcast_to(turned[:, axis : axis + 1], (tile, tile)) for axis in range(4)]
        weights, terms = [], []
        for link in range(LINKS):
            other = nbr_ref[index * LINKS + link]
            rows = table_ref[other]
            terms.append(terms_ref[other])
            power = own[0] * rows[4:5] + own[1] * rows[5:6] + own[2] * rows[6:7]
            power = power + (own[3] + rows[3:4])
            weights.append(jnp.exp2(power).astype(jnp.bfloat16))
        sums = last_dims(jnp.concatenate(terms, axis=1), jnp.concatenate(weights, axis=1))
        sums = sums[0:4] + sums[4:8] + sums[8:12]
        place = pos_ref[:, at]
        speed = vel_ref[:, at]
        force = CONTACT_STIFF * (place * sums[0:1] - sums[1:4])

        cell_x, cell_y = cell_parts(cells_ref[step : step + 1, at], grid_y)
        hit = jnp.where(one_hot(cell_x, grid_x), 1.0, 0.0).astype(jnp.bfloat16)
        lines = jnp.dot(
            field_two_ref[...], jnp.concatenate([hit, hit], axis=0),
            preferred_element_type=jnp.float32,
        )
        pick = one_hot(cell_y, grid_y)
        gravity_x = jnp.sum(jnp.where(pick, lines[:grid_y], 0.0), axis=0, keepdims=True)
        gravity_y = jnp.sum(jnp.where(pick, lines[grid_y:], 0.0), axis=0, keepdims=True)
        accel = jnp.concatenate(
            [
                force[0:1]
                + gravity_x
                + 2.0 * ORBIT_FREQ * speed[1:2]
                + 3.0 * ORBIT_FREQ**2 * (place[0:1] + strip_x),
                force[1:2] + gravity_y - 2.0 * ORBIT_FREQ * speed[0:1],
                force[2:3] - ORBIT_FREQ**2 * (place[2:3] - 0.5),
            ],
            axis=0,
        )
        speed = speed + TIME_STEP * accel
        place = place + TIME_STEP * speed
        return at, place, speed

    def at_of(index):
        return pl.ds(pl.multiple_of(index * tile, tile), tile)

    if not last:

        def body(group, carry):
            for part in range(unroll):
                at, place, speed = one_tile(group * unroll + part)
                pos_out[:, at] = place
                vel_out[:, at] = speed
            return carry

        lax.fori_loop(0, tile_count // unroll, body, 0)
        return

    def shifted(place, strip):
        moved = lax.rem(azi - strip + azi_count + azi_count // 2, azi_count)
        moved = (moved - azi_count // 2).astype(jnp.float32)
        return place + jnp.where(axis_ids == 1, moved, 0.0)

    def body(group, carry):
        for part in range(unroll):
            index = group * unroll + part
            at, place, speed = one_tile(index)
            place = shifted(place, nbr_ref[tile_count * LINKS + index])
            out_ref[:, at_of(target_ref[index])] = jnp.concatenate(
                [place, speed, mass_ref[:, at]], axis=0
            )
        return carry

    lax.fori_loop(0, tile_count // unroll, body, 0)

def advance(step, counts, tile_count, grid_y, slots_out, numbers, slot_ids, target,
            place, speed, mass_row, received, cells, field):
    rad_count, azi_count = counts
    last = step == STEPS - 1
    tile = place.shape[1] // tile_count
    params = pltpu.CompilerParams()
    if last:
        out_shape = jax.ShapeDtypeStruct((7, slots_out * tile), jnp.float32)
        out_specs = VMEM
        more = []
    else:
        out_shape = (jax.ShapeDtypeStruct(place.shape, jnp.float32),) * 2
        out_specs = (VMEM,) * 2
        more = []
    return pl.pallas_call(
        functools.partial(
            step_kernel, step, azi_count, rad_count, tile_count, grid_y, last, UNROLL
        ),
        out_shape=out_shape,
        in_specs=[SMEM] * 3 + [VMEM] * 6,
        out_specs=out_specs,
        scratch_shapes=[
            pltpu.VMEM((tile_count + 4 * EDGE, 8, tile), jnp.float32),
            pltpu.VMEM((tile_count + 4 * EDGE, 16, tile), jnp.bfloat16),
            pltpu.VMEM((field.shape[0], 2 * field.shape[1]), jnp.bfloat16),
        ]
        + more,
        compiler_params=params,
        name=f"advance_{step}",
        cost_estimate=pl.CostEstimate(
            flops=3 * 10**8, bytes_accessed=5 * 10**7, transcendentals=8 * 10**6
        ),
    )(numbers, slot_ids, target, place, speed, mass_row, received, cells, field)


def exact(left, right):
    return jnp.dot(left, right, precision=lax.Precision.HIGHEST)


def solve(density, rad_place, azi_place, rad_count, azi_count):
    _, grid_x, grid_y = density.shape
    size_x, size_y = grid_x * rad_count, grid_y * azi_count
    peers = rad_count * azi_count
    rows = size_y // peers
    basis_x, waves_x = real_basis(size_x)
    basis_y, waves_y = real_basis(size_y)
    slope_y = -0.5 * (np.roll(basis_y, -1, axis=1) - np.roll(basis_y, 1, axis=1))
    table_x = jnp.asarray(basis_x, jnp.float32)
    table_y = jnp.asarray(np.stack([basis_y.T, slope_y.T]), jnp.float32)
    own_y = lax.dynamic_slice_in_dim(table_y, azi_place * grid_y, grid_y, axis=1)
    flat = density.reshape(STEPS * grid_x, grid_y)
    partial = lax.dot_general(
        own_y[0], flat, (((0,), (1,)), ((), ())), precision=lax.Precision.HIGHEST
    )
    partial = partial.reshape(peers, rows, STEPS * grid_x)
    got = lax.all_to_all(partial, ("rad", "azi"), split_axis=0, concat_axis=0, tiled=True)
    lines = got.reshape(rad_count, azi_count, rows, STEPS, grid_x).sum(axis=1)
    lines = jnp.transpose(lines, (2, 1, 0, 3)).reshape(STEPS * rows, size_x)
    spectrum = lax.dot_general(
        lines, table_x, (((1,), (1,)), ((), ())), precision=lax.Precision.HIGHEST
    )
    eigen_x = jnp.asarray(4.0 * np.sin(np.pi * waves_x / size_x) ** 2, jnp.float32)
    eigen_y = jnp.asarray(4.0 * np.sin(np.pi * waves_y / size_y) ** 2, jnp.float32)
    own_eigen = lax.dynamic_slice_in_dim(
        eigen_y, (rad_place * azi_count + azi_place) * rows, rows, axis=0
    )
    total = eigen_x[None, :] + own_eigen[:, None]
    green = jnp.where(total == 0.0, 0.0, -GRAV_SCALE / jnp.where(total == 0.0, 1.0, total))
    spectrum = spectrum.reshape(STEPS, rows, size_x) * green[None]
    lines = exact(spectrum.reshape(STEPS * rows, size_x), table_x).reshape(STEPS, rows, size_x)
    slope = -0.5 * (jnp.roll(lines[0], -1, axis=1) - jnp.roll(lines[0], 1, axis=1))
    sent = jnp.concatenate([slope[None], lines], axis=0)
    sent = sent.reshape(STEPS + 1, rows, rad_count, grid_x)
    sent = jnp.transpose(sent, (2, 1, 0, 3)).reshape(rad_count, 1, rows, (STEPS + 1) * grid_x)
    sent = jnp.broadcast_to(sent, (rad_count, azi_count, rows, (STEPS + 1) * grid_x))
    sent = sent.reshape(peers, rows, (STEPS + 1) * grid_x)
    got = lax.all_to_all(sent, ("rad", "azi"), split_axis=0, concat_axis=0, tiled=True)
    got = got.reshape(size_y, (STEPS + 1) * grid_x)
    field = jnp.concatenate(
        [exact(own_y[0], got[:, :grid_x]), exact(own_y[1], got[:, grid_x : 2 * grid_x])], axis=0
    )
    final = exact(own_y[0], got[:, 2 * grid_x :]).T
    return field, final


def local(
    positions,
    velocities,
    masses,
    neighbours,
    shear_offsets,
    destinations,
    deposit_cells,
    old_potential,
):
    rad_count = lax.axis_size("rad")
    azi_count = lax.axis_size("azi")
    rad_place = lax.axis_index("rad")
    azi_place = lax.axis_index("azi")
    tile_count = neighbours.shape[0]
    tile = positions.shape[1] // tile_count
    grid_x, grid_y = old_potential.shape
    mass_row = masses[None]
    span = EDGE * tile

    def edges_of(place, extra):
        head = jnp.concatenate([place[:, : 4 * span], mass_row[:, : 4 * span]], axis=0)
        sides = [head[:, side * span : (side + 1) * span] for side in (1, 0, 3, 2)]
        edges = jnp.stack(sides)
        if extra is not None:
            lines = [jnp.pad(line, (0, span - line.shape[0])) for line in extra]
            lines = jnp.stack(lines)[:, None]
            edges = jnp.concatenate(
                [edges, lines, jnp.zeros((4, 3, span), jnp.float32)], axis=1
            )
        return edges

    outer = (old_potential[-1], old_potential[0], old_potential[:, -1], old_potential[:, 0])
    counts = (rad_count, azi_count)
    density, received = densities(
        deposit_cells, mass_row, edges_of(positions, outer), counts, grid_x, grid_y
    )
    before = lax.dynamic_index_in_dim(received, azi_place, 0, False)[4, :grid_y]
    after = lax.dynamic_index_in_dim(received, azi_count + azi_place, 0, False)[4, :grid_y]
    left = received[2 * azi_count, 4, :grid_x]
    right = received[2 * azi_count + 1, 4, :grid_x]
    tall = jnp.concatenate([before[None], old_potential, after[None]], axis=0)
    wide = jnp.concatenate([left[:, None], old_potential, right[:, None]], axis=1)
    grad_x = -(tall[2:] - tall[:-2]) * 0.5
    grad_y = -(wide[:, 2:] - wide[:, :-2]) * 0.5
    field = jnp.concatenate([grad_x.T, grad_y.T], axis=0)

    slot_cap = tile_count // 4
    slots_out = slot_cap * azi_count
    tile_ids = jnp.arange(tile_count, dtype=jnp.int32)
    sooner = (tile_ids[None, :] < tile_ids[:, None]) & (
        destinations[None, :] == destinations[:, None]
    )
    rank = jnp.sum(sooner.astype(jnp.int32), axis=1)
    target = destinations * slot_cap + rank
    numbers = jnp.concatenate([neighbours.reshape(-1), destinations])

    def slots_of(step):
        offsets = shear_offsets[step]
        shift_below = offsets[rad_place]
        shift_above = offsets[(rad_place + 1) % rad_count]
        return jnp.stack(
            [
                (azi_place - shift_below) % azi_count,
                azi_count + (azi_place + shift_above) % azi_count,
                jnp.int32(2 * azi_count),
                jnp.int32(2 * azi_count + 1),
            ]
        )

    place, speed = advance(
        0, counts, tile_count, grid_y, slots_out, numbers, slots_of(0), target,
        positions, velocities, mass_row, received, deposit_cells, field,
    )
    field, final = solve(density, rad_place, azi_place, rad_count, azi_count)
    received = exchange(edges_of(place, None), counts, 1)
    packed = advance(
        1, counts, tile_count, grid_y, slots_out, numbers, slots_of(1), target,
        place, speed, mass_row, received, deposit_cells, field,
    )
    return (migrate(packed, azi_count, 2), final)


def solution(mesh):
    placed = (
        P(None, ("rad", "azi")),
        P(None, ("rad", "azi")),
        P(("rad", "azi")),
        P(("rad", "azi"), None),
        P(),
        P(("rad", "azi")),
        P(None, ("rad", "azi")),
        P("rad", "azi"),
    )
    return jax.shard_map(
        local,
        mesh=mesh,
        in_specs=placed,
        out_specs=(P(None, ("rad", "azi")), P("rad", "azi")),
        check_vma=False,
    )
```
